32 devices in a mesh: shot: 8 (over y, x, core), prow: 4 (over z).
Axes of the slice: x: 2, y: 2, z: 4, core: 2. Of those that a mesh axis runs over, the one named last changes fastest.
Arguments:
- queries: bfloat16 [8, 12, 64, 1280], P('shot', 'prow'), may hold values from -120 to 120
- keys: bfloat16 [8, 12, 64, 1280], P('shot', 'prow'), may hold values from -4 to 4
- values: bfloat16 [8, 12, 64, 1280], P('shot', 'prow'), may hold values from -6 to 6
- out_cotangent: bfloat16 [8, 12, 64, 1280], P('shot', 'prow'), may hold values from -3 to 3
- pooled_cotangent: bfloat16 [256, 1280], P(('shot', 'prow')), may hold values from -24 to 24
- box_coords: int32 [256, 4], P(('shot', 'prow')), may hold values from 0 to 64, as said below
- box_shot: int32 [256, 1], P(('shot', 'prow')), may hold values from 0 to 7; in each aligned block of 8 rows (0 to 7, 8 to 15, ...) at most 2 rows name the same one
- position_bias: float32 [16, 49], replicated, may hold values from -2.5 to 2.5
Outputs:
- query_grad: bfloat16 [8, 12, 64, 1280], P('shot', 'prow')
- key_grad: bfloat16 [8, 12, 64, 1280], P('shot', 'prow')
- value_grad: bfloat16 [8, 12, 64, 1280], P('shot', 'prow')
- bias_grad: float32 [16, 49], replicated
The draws below stay inside these ranges and needn't reach their ends.
Inputs may be any that keep to these rules, and one draw needn't show every extreme that they name: `box_shot`: in the rows of one device at most 2 boxes name the same screenshot, a bound that some block reaches of them. `box_coords`: every box has 0 <= r0 < r1 <= 12 and 0 <= c0 < c1 <= 64; it spans 1 to min(8, 12) rows and 1 to min(16, 64) columns.
All inputs are finite; a program needn't handle non-finite values.
Results may differ from the reference program's by a relative error of at most 0.0084.
Values may be sent and summed in bfloat16 or wider, within the bound.
No kernel may reach another device: no remote copies, remote signals or barrier semaphores. Data moves between devices by JAX's collectives and lax.ppermute only.
A program may use at most 128 MiB of HBM per device.

```python
import math
import jax
import jax.numpy as jnp
import numpy as np
from jax import lax

D = 1280
HEADS = 16
HEAD_DIM = 80
WINDOW = 7
CAP = 2
GRID_COLS = 64
SHOTS = 8
GRID_ROWS = 12
BOX_DEV = 8
BOXES = 256
SLOTS = 64


def draw_queries(key, part):
    grid_shape = (SHOTS, GRID_ROWS, GRID_COLS, D)
    drawn = jnp.clip(jax.random.normal(jax.random.fold_in(key, 1), grid_shape, jnp.float32), -4.0, 4.0)
    return drawn.astype(jnp.bfloat16)


def draw_keys(key, part):
    grid_shape = (SHOTS, GRID_ROWS, GRID_COLS, D)
    drawn = jnp.clip(jax.random.normal(jax.random.fold_in(key, 3), grid_shape, jnp.float32), -4.0, 4.0)
    return drawn.astype(jnp.bfloat16)


def draw_box_coords(key, part):
    most_rows = min(8, GRID_ROWS)
    most_cols = min(16, GRID_COLS)
    height = jax.random.randint(jax.random.fold_in(key, 31), (BOXES,), 1, most_rows + 1)
    breadth = jax.random.randint(jax.random.fold_in(key, 32), (BOXES,), 1, most_cols + 1)
    height = height.at[1].set(most_rows)
    breadth = breadth.at[1].set(most_cols)
    top_row = jax.random.randint(jax.random.fold_in(key, 33), (BOXES,), 0, GRID_ROWS - height + 1)
    left_col = jax.random.randint(jax.random.fold_in(key, 34), (BOXES,), 0, GRID_COLS - breadth + 1)
    top_row = top_row.at[0].set(GRID_ROWS - height[0])
    left_col = left_col.at[0].set(GRID_COLS - breadth[0])
    return jnp.stack([top_row, top_row + height, left_col, left_col + breadth], axis=1).astype(jnp.int32)


def shard_levels(rng, shape, cuts, low, largest):
    gain = 1.0
    for dim, blocks in cuts:
        heights = jax.random.uniform(jax.random.fold_in(jax.random.fold_in(rng, 6), dim), (blocks,), jnp.float32, low / len(cuts), largest / len(cuts))
        gain = gain * jnp.repeat(jnp.exp(heights), shape[dim] // blocks).reshape((-1,) + (1,) * (len(shape) - 1 - dim))
    return gain


def shared_out(key, own, number, rows, amount, top, limit, slope):
    ranking = jax.random.permutation(key, amount)
    heavy_load, common = load_shares(amount, rows * top, limit, slope, True), load_shares(amount, rows * top, limit, slope, False)
    places = jnp.arange(amount)

    def named(lengths, rotation):
        used = int((lengths > 0).sum())
        fixed = max(1, used // 4)
        moved = fixed + (places - fixed + rotation * (used - fixed)) % max(1, amount - fixed)
        return jnp.zeros((amount,), jnp.int32).at[ranking[jnp.where(places < fixed, places, moved)]].set(jnp.asarray(lengths, jnp.int32))

    lengths = jnp.where(number % 4 == 0, named(heavy_load, number // 4), named(common, number - number // 4 - 1))
    mixed = jax.random.permutation(jax.random.fold_in(own, 3), amount)
    source_of, taker = mixed[0:amount // 2 * 2:2], mixed[1:amount // 2 * 2:2]
    room = jnp.minimum(lengths[source_of] - 1, limit - lengths[taker]) // 2
    room = jnp.where((source_of == ranking[0]) | (taker == ranking[0]) | (lengths[taker] == 0), 0, jnp.maximum(room, 0))
    moved = jax.random.randint(jax.random.fold_in(own, 4), (amount // 2,), 0, 1 << 20) % (room + 1)
    lengths = lengths.at[source_of].add(-moved).at[taker].add(moved)
    items = jnp.searchsorted(jnp.cumsum(lengths), jnp.arange(rows * top), side="right").astype(jnp.int32)
    grid = items.reshape(top, rows).T
    grid = grid[jax.random.permutation(jax.random.fold_in(own, 1), rows)]
    rotation = jax.random.randint(jax.random.fold_in(own, 2), (rows, 1), 0, top)
    return jnp.take_along_axis(grid, (jnp.arange(top)[None, :] + rotation) % top, axis=1)


def load_shares(number_of, total, limit, skew, full):
    weights = [(1 << 20) // math.isqrt(grade ** skew) + 1 for grade in range(1, number_of + 1)]
    largest = limit if full else min(limit, max(-(-total // number_of), total * weights[0] // sum(weights)))
    least = 1 if total - largest >= number_of - 1 else 0
    given, surplus = [largest] + [least] * (number_of - 1), total - largest - least * (number_of - 1)
    while surplus > 0:
        movable = [i for i in range(1, number_of) if given[i] < largest] or [i for i in range(1, number_of) if given[i] < limit]
        mass, budget = sum([weights[i] for i in movable]), surplus
        for i in movable:
            more = min(limit - given[i], max(1, budget * weights[i] // mass), surplus)
            given[i] = given[i] + more
            surplus = surplus - more
    return np.array(given)


def bell_draw(rng, dims, scale, most, split=(), kind=jnp.bfloat16):
    array = jax.random.normal(rng, dims, jnp.float32) * scale
    if len(split) > 0:
        array = shard_levels(rng, dims, split, -0.22, 0.18) * array
    return jnp.clip(array, min=-most, max=most).astype(kind)


def setup_inputs(seed: int = 0) -> dict:
    streams_of = jax.random.split(jax.random.key(seed), 9)
    queries = draw_queries(jax.random.fold_in(streams_of[8], 71), 0)
    keys = draw_keys(jax.random.fold_in(streams_of[8], 71), 0)
    values = bell_draw(streams_of[2], (SHOTS, GRID_ROWS, GRID_COLS, D), 1.0, 6.0, ((0, 8), (1, 4)))
    out_cotangent = bell_draw(streams_of[3], (SHOTS, GRID_ROWS, GRID_COLS, D), 0.5, 3.0, ((0, 8), (1, 4)))
    pooled_cotangent = bell_draw(streams_of[4], (BOXES, D), 4.0, 24.0, ((0, 32),))
    box_coords = draw_box_coords(jax.random.fold_in(streams_of[8], 71), 0)
    box_shot_keys = jax.random.split(jax.random.fold_in(streams_of[6], 1), BOXES // BOX_DEV)
    box_shot_turns = jax.random.permutation(jax.random.fold_in(streams_of[6], 3), BOXES // BOX_DEV)
    box_shot = jax.vmap(lambda own, number: shared_out(jax.random.fold_in(streams_of[6], 2), own, number, BOX_DEV, SHOTS, 1, CAP, 2))(box_shot_keys, box_shot_turns).reshape((BOXES, 1))
    position_bias = bell_draw(streams_of[7], (HEADS, WINDOW * WINDOW), 0.5, 2.5, (), jnp.float32)
    return dict(queries=queries, keys=keys, values=values, out_cotangent=out_cotangent, pooled_cotangent=pooled_cotangent, box_coords=box_coords, box_shot=box_shot, position_bias=position_bias)


def pool_shot(shot_index, pooled_cotangent, box_coords, box_order, counts, starts):
    slot_index = jnp.arange(SLOTS, dtype=jnp.int32)
    box_index = jnp.clip(starts[shot_index] + slot_index, 0, BOXES - 1).astype(jnp.int32)
    chosen = box_order[box_index]
    is_valid = (slot_index < counts[shot_index]).astype(jnp.float32)
    corner = box_coords[chosen]
    box_area = ((corner[:, 1] - corner[:, 0]) * (corner[:, 3] - corner[:, 2])).astype(jnp.float32)
    weight_low = lax.optimization_barrier((1.0 / box_area).astype(jnp.bfloat16))
    weight = weight_low.astype(jnp.float32) * is_valid
    box_values = pooled_cotangent[chosen].astype(jnp.float32) * weight[:, None]
    corners_sum = jnp.zeros((GRID_ROWS + 1, GRID_COLS + 1, D), jnp.float32)
    corners_sum = corners_sum.at[corner[:, 0], corner[:, 2]].add(box_values)
    corners_sum = corners_sum.at[corner[:, 0], corner[:, 3]].add(-box_values)
    corners_sum = corners_sum.at[corner[:, 1], corner[:, 2]].add(-box_values)
    corners_sum = corners_sum.at[corner[:, 1], corner[:, 3]].add(box_values)
    return jnp.cumsum(jnp.cumsum(corners_sum, axis=0), axis=1)[:GRID_ROWS, :GRID_COLS]


def shot_grads(query, key_tile, value_tile, cotangent, position_bias):
    half_window = WINDOW // 2
    score_scale = HEAD_DIM ** -0.5
    head_shape = (GRID_ROWS, GRID_COLS, HEADS, HEAD_DIM)
    query_wide = query.reshape(head_shape).astype(jnp.float32)
    key_wide = key_tile.reshape(head_shape).astype(jnp.float32)
    value_wide = value_tile.reshape(head_shape).astype(jnp.float32)
    cot_wide = cotangent.reshape(head_shape).astype(jnp.float32)
    pad_spec = ((half_window, half_window), (half_window, half_window), (0, 0), (0, 0))
    key_padded = jnp.pad(key_wide, pad_spec)
    value_padded = jnp.pad(value_wide, pad_spec)
    row_index = jnp.arange(GRID_ROWS, dtype=jnp.int32)[:, None]
    col_index = jnp.arange(GRID_COLS, dtype=jnp.int32)[None, :]
    score_list = []
    inside_list = []
    for i in range(WINDOW):
        for j in range(WINDOW):
            shifted = key_padded[i:i + GRID_ROWS, j:j + GRID_COLS]
            score_term = jnp.sum(query_wide * shifted, axis=-1) * score_scale + position_bias[:, i * WINDOW + j]
            score_list.append(score_term)
            inside = (row_index + i - half_window >= 0) & (row_index + i - half_window < GRID_ROWS)
            inside = inside & (col_index + j - half_window >= 0) & (col_index + j - half_window < GRID_COLS)
            inside_list.append(inside[:, :, None])
    scores = jnp.stack(score_list, axis=0)
    inside_all = jnp.stack(inside_list, axis=0)
    row_peak = jnp.max(jnp.where(inside_all, scores, -jnp.inf), axis=0)
    exponent = jnp.where(inside_all, jnp.exp(scores - row_peak), 0.0)
    weights_full = exponent / jnp.sum(exponent, axis=0)
    prob_low = lax.optimization_barrier(weights_full.astype(jnp.bfloat16)).astype(jnp.float32)
    attended = jnp.zeros(head_shape, jnp.float32)
    grad_list = []
    for i in range(WINDOW):
        for j in range(WINDOW):
            shifted = value_padded[i:i + GRID_ROWS, j:j + GRID_COLS]
            attended = attended + prob_low[i * WINDOW + j][..., None] * shifted
            grad_list.append(jnp.sum(cot_wide * shifted, axis=-1))
    row_delta = jnp.sum(cot_wide * attended, axis=-1)
    prob_grad = jnp.stack(grad_list, axis=0)
    score_grad = weights_full * (prob_grad - row_delta[None])
    score_low = lax.optimization_barrier(score_grad.astype(jnp.bfloat16)).astype(jnp.float32)
    query_grad = jnp.zeros(head_shape, jnp.float32)
    key_grad = jnp.zeros(key_padded.shape, jnp.float32)
    value_grad = jnp.zeros(value_padded.shape, jnp.float32)
    for i in range(WINDOW):
        for j in range(WINDOW):
            offset = i * WINDOW + j
            shifted = key_padded[i:i + GRID_ROWS, j:j + GRID_COLS]
            query_grad = query_grad + score_low[offset][..., None] * shifted
            key_grad = key_grad.at[i:i + GRID_ROWS, j:j + GRID_COLS].add(score_low[offset][..., None] * query_wide)
            value_grad = value_grad.at[i:i + GRID_ROWS, j:j + GRID_COLS].add(prob_low[offset][..., None] * cot_wide)
    flat_shape = (GRID_ROWS, GRID_COLS, D)
    query_out = (query_grad * score_scale).reshape(flat_shape).astype(jnp.bfloat16)
    key_out = (key_grad[half_window:half_window + GRID_ROWS, half_window:half_window + GRID_COLS] * score_scale).reshape(flat_shape).astype(jnp.bfloat16)
    value_out = value_grad[half_window:half_window + GRID_ROWS, half_window:half_window + GRID_COLS].reshape(flat_shape).astype(jnp.bfloat16)
    bias_part = jnp.transpose(jnp.sum(score_grad, axis=(1, 2)))
    return query_out, key_out, value_out, bias_part


def reference(queries, keys, values, out_cotangent, pooled_cotangent, box_coords, box_shot, position_bias):
    shot_ids = box_shot[:, 0]
    box_order = jnp.argsort(shot_ids, stable=True).astype(jnp.int32)
    counts = jnp.sum((shot_ids[:, None] == jnp.arange(SHOTS, dtype=jnp.int32)[None, :]).astype(jnp.int32), axis=0)
    starts = (jnp.cumsum(counts) - counts).astype(jnp.int32)

    def per_shot(shot_index):
        box_term = pool_shot(shot_index, pooled_cotangent, box_coords, box_order, counts, starts)
        cotangent = (out_cotangent[shot_index].astype(jnp.float32) + box_term).astype(jnp.bfloat16)
        return shot_grads(queries[shot_index], keys[shot_index], values[shot_index], cotangent, position_bias)

    query_grad, key_grad, value_grad, bias_parts = lax.map(per_shot, jnp.arange(SHOTS, dtype=jnp.int32))
    return query_grad, key_grad, value_grad, jnp.sum(bias_parts, axis=0)
```

```python
import functools
import math

import jax
import jax.numpy as jnp
import numpy as np
from jax import lax
from jax.experimental import pallas as pl
from jax.experimental.pallas import tpu as pltpu
from jax.sharding import PartitionSpec as P

WINDOW = 7
HALF = WINDOW // 2
CAP = 2
LANES = 128
COL_BLOCK = 16
SHIFT = 4
KEY_COLS = COL_BLOCK + 2 * SHIFT
MASKED = -1e30
F32 = jnp.float32
BF16 = jnp.bfloat16
VMEM_LIMIT = 60 * 1024 * 1024

NT = (((1,), (1,)), ((), ()))
NN = (((1,), (0,)), ((), ()))
TN = (((0,), (0,)), ((), ()))


def dot(a, b, dims):
    return lax.dot_general(a, b, dims, preferred_element_type=F32)


class Plan:
    def __init__(self, rows, cols, head_size):
        self.rows, self.cols, self.head_size = rows, cols, head_size
        self.features = math.lcm(head_size, LANES)
        self.heads = self.features // head_size
        self.queries = rows * COL_BLOCK
        self.lanes = self.heads * self.queries
        assert cols % COL_BLOCK == 0 and self.lanes % LANES == 0 and rows >= HALF
        self.key_rows = rows + 2 * HALF
        self.keys = self.key_rows * KEY_COLS
        self.wide_cols = cols + 2 * SHIFT
        self.blocks = cols // COL_BLOCK
        self.tiles = self.lanes // LANES
        self.feature_tiles = self.features // LANES

    def window(self, head):
        start = head * self.head_size
        return start // LANES, -(-(start + self.head_size) // LANES)

    def heads_of(self, tile):
        first = tile * LANES // self.queries
        last = ((tile + 1) * LANES - 1) // self.queries
        return range(first, last + 1)

    def tile_window(self, tile):
        heads = self.heads_of(tile)
        return self.window(heads[0])[0] * LANES, self.window(heads[-1])[1] * LANES

    def feature_chunks(self):
        chunks = []
        for low in range(0, self.features, 2 * LANES):
            high = min(low + 2 * LANES, self.features)
            reached = [
                tile
                for tile in range(self.tiles)
                if self.tile_window(tile)[0] < high and self.tile_window(tile)[1] > low
            ]
            chunks.append((low, high, reached[0] * LANES, (reached[-1] + 1) * LANES))
        return chunks


def head_mask(plan):
    feature = np.arange(plan.features)
    rows = [(feature // plan.head_size == head).astype(np.float32) for head in range(plan.heads)]
    return jnp.asarray(np.repeat(np.stack(rows), 16, axis=0), BF16)


def lane_tables(plan):
    lane = np.arange(plan.lanes)
    row = (lane // COL_BLOCK) % plan.rows
    col = lane % COL_BLOCK
    table = np.zeros((8, plan.lanes), np.int32)
    table[0], table[1] = row, col
    return jnp.asarray(table)


def head_sum(plan):
    lane = np.arange(plan.lanes)
    return jnp.asarray(
        (lane[None, :] // plan.queries == np.arange(plan.heads)[:, None]).astype(np.float32)
    )


def grads_kernel(
    plan, where_ref, bias_ref, lane_ref, mask_ref, sum_ref, q_ref, k_ref, v_ref, cot_ref, one_ref,
    two_ref, dq_ref, own_ref, out_one_ref, out_two_ref, bias_out_ref, kpad, vpad, dk, dv, kblk,
    vblk, qbd, obd, pblk, sblk, table, acc, offs,
):
    rows, cols, feats = plan.rows, plan.cols, plan.features
    scale = plan.head_size ** (-0.5)
    row_start, height, odd = where_ref[0], where_ref[1], where_ref[2]
    mid = slice(SHIFT, SHIFT + cols)
    for pad in (kpad, vpad):
        pad[:, :SHIFT, :] = jnp.zeros((plan.key_rows, SHIFT, feats), F32)
        pad[:, SHIFT + cols :, :] = jnp.zeros((plan.key_rows, SHIFT, feats), F32)
    kpad[HALF : HALF + rows, mid, :] = k_ref[0].astype(F32)
    vpad[HALF : HALF + rows, mid, :] = v_ref[0].astype(F32)

    def fill(above_ref, below_ref):
        kpad[:HALF, mid, :] = above_ref[:, :, :feats].astype(F32)
        vpad[:HALF, mid, :] = above_ref[:, :, feats:].astype(F32)
        kpad[HALF + rows :, mid, :] = below_ref[:, :, :feats].astype(F32)
        vpad[HALF + rows :, mid, :] = below_ref[:, :, feats:].astype(F32)

    @pl.when(odd == 0)
    def _():
        fill(two_ref, one_ref)

    @pl.when(odd == 1)
    def _():
        fill(one_ref, two_ref)

    dk[...] = jnp.zeros_like(dk)
    dv[...] = jnp.zeros_like(dv)
    qbd[...] = jnp.zeros_like(qbd)
    obd[...] = jnp.zeros_like(obd)
    acc[...] = jnp.zeros_like(acc)

    key_col = lax.broadcasted_iota(jnp.int32, (KEY_COLS, LANES), 0)
    for tile in range(plan.tiles):
        at = slice(tile * LANES, (tile + 1) * LANES)
        lane_row = jnp.broadcast_to(lane_ref[0:1, at], (KEY_COLS, LANES))
        lane_col = jnp.broadcast_to(lane_ref[1:2, at], (KEY_COLS, LANES))
        shift = key_col - lane_col - (SHIFT - HALF)
        by_row = []
        for i in range(WINDOW):
            part = jnp.full((KEY_COLS, LANES), MASKED, F32)
            for j in range(WINDOW):
                o = i * WINDOW + j
                part = jnp.where(
                    shift == j, jnp.broadcast_to(bias_ref[o : o + 1, at], part.shape), part
                )
            by_row.append(part)
        for key_row in range(plan.key_rows):
            part = jnp.full((KEY_COLS, LANES), MASKED, F32)
            for row in range(rows):
                if 0 <= key_row - row < WINDOW:
                    part = jnp.where(lane_row == row, by_row[key_row - row], part)
            place = row_start + key_row - HALF
            inside = jnp.logical_and(place >= 0, place < height)
            part = part + jnp.where(inside, 0.0, MASKED)
            table[key_row * KEY_COLS : (key_row + 1) * KEY_COLS, at] = part

    feature_lane = lax.broadcasted_iota(jnp.int32, (COL_BLOCK, LANES), 1)
    key_iota = lax.broadcasted_iota(jnp.int32, (plan.key_rows, KEY_COLS, LANES), 1)
    for block in range(plan.blocks):
        base = block * COL_BLOCK
        kblk[...] = kpad[:, base : base + KEY_COLS, :].reshape(plan.keys, feats).astype(BF16)
        vblk[...] = vpad[:, base : base + KEY_COLS, :].reshape(plan.keys, feats).astype(BF16)
        for head in range(plan.heads):
            low, high = plan.window(head)
            for row in range(rows):
                start = head * plan.queries + row * COL_BLOCK
                at = (slice(start, start + COL_BLOCK), slice(low * LANES, high * LANES))
                mask = mask_ref[head * 16 : head * 16 + COL_BLOCK, low * LANES : high * LANES]
                grid_at = (0, row, slice(base, base + COL_BLOCK), slice(low * LANES, high * LANES))
                qbd[at] = q_ref[grid_at] * mask
                obd[at] = cot_ref[grid_at] * mask
        edge = None
        if block == 0 or block == plan.blocks - 1:
            place = key_iota + (base - SHIFT)
            edge = jnp.where(jnp.logical_and(place >= 0, place < cols), 0.0, MASKED)
            edge = edge.reshape(plan.keys, LANES)
        dq_tiles = []
        for tile in range(plan.tiles):
            at = slice(tile * LANES, (tile + 1) * LANES)
            low, high = plan.tile_window(tile)
            scores = dot(kblk[:, low:high], qbd[at, low:high], NT) * scale + table[:, at]
            if edge is not None:
                scores = scores + edge
            exponent = jnp.exp(scores - jnp.max(scores, axis=0, keepdims=True))
            probs = exponent * (1.0 / jnp.sum(exponent, axis=0, keepdims=True))
            prob_low = probs.astype(BF16)
            prob_grad = dot(vblk[:, low:high], obd[at, low:high], NT)
            row_delta = jnp.sum(prob_low.astype(F32) * prob_grad, axis=0, keepdims=True)
            score_grad = probs * (prob_grad - row_delta)
            acc[:, at] += score_grad
            score_low = score_grad.astype(BF16)
            pblk[:, at] = prob_low
            sblk[:, at] = score_low
            dq_tiles.append(dot(score_low, kblk[:, low:high], TN))
        for low, high, first, last in plan.feature_chunks():
            shape = (plan.key_rows, KEY_COLS, high - low)
            part = dot(sblk[:, first:last], qbd[first:last, low:high], NN)
            dk[:, base : base + KEY_COLS, low:high] += part.reshape(shape)
            part = dot(pblk[:, first:last], obd[first:last, low:high], NN)
            dv[:, base : base + KEY_COLS, low:high] += part.reshape(shape)
        for row in range(rows):
            for ft in range(plan.feature_tiles):
                total = None
                for head in range(plan.heads):
                    low, high = plan.window(head)
                    if not low <= ft < high:
                        continue
                    start = head * plan.queries + row * COL_BLOCK
                    tile = start // LANES
                    begin = plan.tile_window(tile)[0]
                    piece = dq_tiles[tile][
                        start - tile * LANES : start - tile * LANES + COL_BLOCK,
                        ft * LANES - begin : (ft + 1) * LANES - begin,
                    ]
                    lo = head * plan.head_size - ft * LANES
                    keep = jnp.logical_and(
                        feature_lane >= lo, feature_lane < lo + plan.head_size
                    )
                    total = jnp.where(keep, piece, 0.0 if total is None else total)
                dq_ref[0, row, base : base + COL_BLOCK, ft * LANES : (ft + 1) * LANES] = (
                    total * scale
                ).astype(BF16)

    own_ref[:, :, :feats] = dk[HALF : HALF + rows, mid, :] * scale
    own_ref[:, :, feats:] = dv[HALF : HALF + rows, mid, :]

    def send(above_ref, below_ref):
        above_ref[:, :, :feats] = (dk[:HALF, mid, :] * scale).astype(BF16)
        above_ref[:, :, feats:] = dv[:HALF, mid, :].astype(BF16)
        below_ref[:, :, :feats] = (dk[HALF + rows :, mid, :] * scale).astype(BF16)
        below_ref[:, :, feats:] = dv[HALF + rows :, mid, :].astype(BF16)

    @pl.when(odd == 0)
    def _():
        send(out_two_ref, out_one_ref)

    @pl.when(odd == 1)
    def _():
        send(out_one_ref, out_two_ref)

    offs[...] = jnp.zeros_like(offs)
    for tile in range(plan.tiles):
        at = slice(tile * LANES, (tile + 1) * LANES)
        lane_row = jnp.broadcast_to(lane_ref[0:1, at], (KEY_COLS, LANES))
        lane_col = jnp.broadcast_to(lane_ref[1:2, at], (KEY_COLS, LANES))
        shift = key_col - lane_col - (SHIFT - HALF)
        for i in range(WINDOW):
            part = None
            for row in range(rows):
                key_row = row + i
                piece = acc[key_row * KEY_COLS : (key_row + 1) * KEY_COLS, at]
                part = piece if part is None else jnp.where(lane_row == row, piece, part)
            for j in range(WINDOW):
                o = i * WINDOW + j
                offs[o : o + 1, at] = jnp.sum(
                    jnp.where(shift == j, part, 0.0), axis=0, keepdims=True
                )
    bias_out_ref[...] = lax.dot_general(
        sum_ref[...], offs[...], NT, precision=lax.Precision.HIGHEST, preferred_element_type=F32
    )


def group_grads(plan, group, where, bias_wide, queries, keys, values, cotangent, one, two, dq):
    feats = plan.features
    rows, cols = plan.rows, plan.cols
    block = pl.BlockSpec((1, rows, cols, feats), lambda i: (0, 0, 0, group))

    def whole(shape):
        return pl.BlockSpec(shape, lambda i: (0,) * len(shape))

    halo = (HALF, cols, 2 * feats)
    offsets = bias_wide.shape[0]
    padded = (plan.key_rows, plan.wide_cols, feats)
    lanes = plan.lanes
    constants = (lane_tables(plan), head_mask(plan), head_sum(plan))
    args = [where, bias_wide, *constants, queries, keys, values, cotangent, one, two]
    in_specs = [
        pl.BlockSpec(memory_space=pltpu.SMEM),
        pl.BlockSpec((offsets, lanes), lambda i: (0, group)),
        *[whole(c.shape) for c in constants],
        block, block, block, block, whole(halo), whole(halo),
    ]
    kernel = functools.partial(grads_kernel, plan)
    aliases = {}
    if dq is not None:
        aliases = {len(args): 0}
        position = len(args)
        args.append(dq)
        in_specs.append(pl.BlockSpec(memory_space=pl.ANY))
        inner = kernel

        def kernel(*refs):
            return inner(*refs[:position], *refs[position + 1 :])

    return pl.pallas_call(
        kernel,
        grid=(1,),
        in_specs=in_specs,
        out_specs=[
            block, whole((rows, cols, 2 * feats)), whole(halo), whole(halo),
            whole((plan.heads, offsets)),
        ],
        out_shape=[
            jax.ShapeDtypeStruct(queries.shape, BF16),
            jax.ShapeDtypeStruct((rows, cols, 2 * feats), F32),
            jax.ShapeDtypeStruct(halo, BF16),
            jax.ShapeDtypeStruct(halo, BF16),
            jax.ShapeDtypeStruct((plan.heads, offsets), F32),
        ],
        scratch_shapes=[
            pltpu.VMEM(padded, F32), pltpu.VMEM(padded, F32),
            pltpu.VMEM(padded, F32), pltpu.VMEM(padded, F32),
            pltpu.VMEM((plan.keys, feats), BF16), pltpu.VMEM((plan.keys, feats), BF16),
            pltpu.VMEM((lanes, feats), BF16), pltpu.VMEM((lanes, feats), BF16),
            pltpu.VMEM((plan.keys, lanes), BF16), pltpu.VMEM((plan.keys, lanes), BF16),
            pltpu.VMEM((plan.keys, lanes), F32), pltpu.VMEM((plan.keys, lanes), F32),
            pltpu.VMEM((offsets, lanes), F32),
        ],
        input_output_aliases=aliases,
        compiler_params=pltpu.CompilerParams(vmem_limit_bytes=VMEM_LIMIT),
        cost_estimate=pl.CostEstimate(
            flops=10 * plan.blocks * plan.keys * lanes * 256,
            transcendentals=plan.blocks * plan.keys * lanes,
            bytes_accessed=10 * rows * cols * feats * 2,
        ),
        name="band_grads",
    )(*args)


def route_kernel(shots, lists, per_list, width, box_ref, out_ref):
    boxes = lists * per_list
    payload = box_ref[...]
    target = payload[:, width + 4 : width + 5].astype(F32)
    shot_lane = lax.broadcasted_iota(jnp.int32, (boxes, shots), 1).astype(F32)
    member = (target == shot_lane).astype(F32)
    row = lax.broadcasted_iota(jnp.int32, (boxes, boxes), 0)
    col = lax.broadcasted_iota(jnp.int32, (boxes, boxes), 1)
    own_list = lax.broadcasted_iota(jnp.int32, (boxes, 1), 0)
    list_of = jnp.zeros((boxes, 1), jnp.int32)
    first_of = jnp.zeros((boxes, boxes), jnp.bool_)
    for number in range(lists):
        inside_col = (own_list >= number * per_list) & (own_list < (number + 1) * per_list)
        list_of = jnp.where(inside_col, number, list_of)
        inside = (row >= number * per_list) & (row < (number + 1) * per_list)
        first_of = first_of | (inside & (col >= number * per_list))
    before = (first_of & (col < row)).astype(F32)
    earlier = dot(before.astype(BF16), member.astype(BF16), NN)
    rank = jnp.sum(earlier * member, axis=1, keepdims=True)
    slot = target * (lists * CAP) + list_of.astype(F32) * CAP + rank
    slots = shots * lists * CAP
    slot_lane = lax.broadcasted_iota(jnp.int32, (boxes, slots), 1).astype(F32)
    placing = (slot == slot_lane).astype(F32).astype(BF16)
    out_ref[...] = dot(placing, payload, TN).astype(BF16)


def route_boxes(payload, shots, lists, per_list, width):
    return pl.pallas_call(
        functools.partial(route_kernel, shots, lists, per_list, width),
        out_shape=jax.ShapeDtypeStruct((shots * lists * CAP, payload.shape[1]), BF16),
        compiler_params=pltpu.CompilerParams(vmem_limit_bytes=VMEM_LIMIT),
        name="route_boxes",
    )(payload)


def cotangent_kernel(width, where_ref, slot_ref, base_ref, out_ref):
    slots = slot_ref.shape[0]
    _, rows, cols, _ = base_ref.shape
    corner = slot_ref[:, width : width + LANES].astype(F32)
    r0, r1, c0, c1 = (corner[:, i : i + 1] for i in range(4))
    area = jnp.maximum((r1 - r0) * (c1 - c0), 1.0)
    weight = (1.0 / area).astype(BF16).astype(F32)
    col = lax.broadcasted_iota(jnp.int32, (slots, cols), 1).astype(F32)
    in_cols = (c0 <= col) & (col < c1)
    values = slot_ref[:, :width]
    for row in range(rows):
        place = (where_ref[0] + row).astype(F32)
        in_row = (r0 <= place) & (place < r1)
        pool = jnp.where(in_cols & in_row, weight, 0.0).astype(BF16)
        term = dot(pool, values, TN)
        out_ref[0, row] = (base_ref[0, row].astype(F32) + term).astype(BF16)


def add_boxes(where, slots, out_cotangent):
    width = out_cotangent.shape[3]
    return pl.pallas_call(
        functools.partial(cotangent_kernel, width),
        in_specs=[
            pl.BlockSpec(memory_space=pltpu.SMEM),
            pl.BlockSpec(memory_space=pltpu.VMEM),
            pl.BlockSpec(memory_space=pltpu.VMEM),
        ],
        out_specs=pl.BlockSpec(memory_space=pltpu.VMEM),
        out_shape=jax.ShapeDtypeStruct(out_cotangent.shape, BF16),
        compiler_params=pltpu.CompilerParams(vmem_limit_bytes=VMEM_LIMIT),
        name="add_boxes",
    )(where, slots, out_cotangent)


def join_kernel(feats, groups, *refs):
    ins, (dk_ref, dv_ref) = refs[:-2], refs[-2:]
    for group in range(groups):
        own, one, two = ins[3 * group : 3 * group + 3]
        low = group * feats
        for ref, begin in ((dk_ref, 0), (dv_ref, feats)):
            at = (slice(None), slice(None), slice(begin, begin + feats))
            total = own[at] + one[at].astype(F32) + two[at].astype(F32)
            ref[0, :, :, low : low + feats] = total.astype(BF16)


def join_grads(feats, parts, shape):
    flat = [a for part in parts for a in part]
    return pl.pallas_call(
        functools.partial(join_kernel, feats, len(parts)),
        in_specs=[pl.BlockSpec(memory_space=pltpu.VMEM)] * len(flat),
        out_specs=[pl.BlockSpec(memory_space=pltpu.VMEM)] * 2,
        out_shape=[jax.ShapeDtypeStruct(shape, BF16)] * 2,
        compiler_params=pltpu.CompilerParams(vmem_limit_bytes=VMEM_LIMIT),
        name="join_grads",
    )(*flat)


def swap_pairs(count, first):
    pairs = [(i, i + 1) for i in range(first, count - 1, 2)]
    return pairs + [(j, i) for i, j in pairs]


def per_device(
    queries, keys, values, out_cotangent, pooled_cotangent, box_coords, box_shot, position_bias
):
    shots = lax.axis_size("shot")
    prows = lax.axis_size("prow")
    _, rows, cols, width = queries.shape
    heads = position_bias.shape[0]
    plan = Plan(rows, cols, width // heads)
    assert rows == HALF and width % plan.features == 0
    groups = width // plan.features
    feats = plan.features
    me = lax.axis_index("prow")
    where = jnp.stack([me * rows, jnp.int32(rows * prows), me % 2, jnp.int32(0)]).astype(jnp.int32)

    per_list = pooled_cotangent.shape[0]
    extra = jnp.concatenate([box_coords, box_shot], axis=1).astype(BF16)
    extra = jnp.pad(extra, ((0, 0), (0, LANES - extra.shape[1])))
    payload = jnp.concatenate([pooled_cotangent, extra], axis=1)
    lists = [payload]
    for step in range(1, prows):
        turn = [(i, (i + step) % prows) for i in range(prows)]
        lists.append(lax.ppermute(payload, "prow", turn))
    payloads = jnp.concatenate(lists, axis=0)

    halos = []
    for group in range(groups):
        at = slice(group * feats, (group + 1) * feats)
        paired = jnp.concatenate([keys[0, :, :, at], values[0, :, :, at]], axis=2)
        halos.append(
            [lax.ppermute(paired, "prow", swap_pairs(prows, first)) for first in (0, 1)]
        )

    routed = route_boxes(payloads, shots, prows, per_list, width)
    slots = lax.all_to_all(routed, "shot", split_axis=0, concat_axis=0, tiled=True)
    cotangent = add_boxes(where, slots, out_cotangent)

    offsets = -(-(WINDOW * WINDOW) // 8) * 8
    bias_wide = jnp.broadcast_to(
        position_bias.T[:, :, None], (WINDOW * WINDOW, heads, plan.queries)
    ).reshape(WINDOW * WINDOW, heads * plan.queries)
    bias_wide = jnp.pad(bias_wide, ((0, offsets - WINDOW * WINDOW), (0, 0)))

    dq = None
    parts, bias_parts = [], []
    for group in range(groups):
        one, two = halos[group]
        dq, own, send_one, send_two, bias_part = group_grads(
            plan, group, where, bias_wide, queries, keys, values, cotangent, one, two, dq
        )
        got_one = lax.ppermute(send_one, "prow", swap_pairs(prows, 0))
        got_two = lax.ppermute(send_two, "prow", swap_pairs(prows, 1))
        parts.append((own, got_one, got_two))
        bias_parts.append(bias_part)
    dk, dv = join_grads(feats, parts, queries.shape)

    bias = jnp.concatenate(bias_parts, axis=0)
    bias = jnp.broadcast_to(bias[None], (shots, *bias.shape))
    bias = jnp.sum(lax.all_to_all(bias, "shot", split_axis=0, concat_axis=0, tiled=True), axis=0)
    step = 1
    while step < prows:
        bias = bias + lax.ppermute(bias, "prow", [(i, i ^ step) for i in range(prows)])
        step *= 2
    return dq, dk, dv, bias[:, : WINDOW * WINDOW]


def solution(mesh):
    grid = P("shot", "prow", None, None)
    box = P(("shot", "prow"), None)
    return jax.shard_map(
        per_device,
        mesh=mesh,
        in_specs=(grid, grid, grid, grid, box, box, box, P()),
        out_specs=(grid, grid, grid, P()),
        check_vma=False,
    )
```
